32 devices in a mesh: row: 8 (over y, x, core), col: 4 (over z).
Axes of the slice: x: 2, y: 2, z: 4, core: 2. Of those that a mesh axis runs over, the one named last changes fastest.
Arguments:
- features: bfloat16 [4096, 1024], P(('row', 'col')), may hold values from -6 to 6
- node_valid: int32 [32, 128], P(('row', 'col')), may hold values 0 or 1
- self_mask: int32 [32, 128, 128], P(('row', 'col')), may hold values 0 or 1
- pair_blocks: int32 [8, 4, 8, 2], P('row', 'col'), may hold values from 0 to 31, as said below
- pair_count: int32 [8, 4], P('row', 'col'), may hold values from 0 to 8, as said below
- pair_masks: int32 [8, 4, 8, 128, 128], P('row', 'col'), may hold values 0 or 1
- weight_src: bfloat16 [1024, 1024], replicated, may hold values from -0.1875 to 0.1875
- weight_tgt: bfloat16 [1024, 1024], replicated, may hold values from -0.1875 to 0.1875
- attn: float32 [4, 256], replicated
- bias: float32 [1024], replicated, may hold values from -6 to 6
Outputs:
- attended: bfloat16 [4096, 1024], P(('row', 'col'))
The draws below stay inside these ranges and needn't reach their ends.
Inputs may be any that keep to these rules, and one draw needn't show every extreme that they name: `pair_blocks`: cell (r, c) lists in each slot a pair (i, j) of different blocks: i is held by a device of grid row r and j by a device of grid column c, block b being held by device b // 1 counted row by row. No unordered pair stands in two live slots. Slots from pair_count on are not used. Some cell has all 8 slots live.
All inputs are finite; a program needn't handle non-finite values. No bound on the sum of `node_valid` or of `self_mask` or of `pair_masks` on one device may be relied on, other than what follows from the above.
Results may differ from the reference program's by a relative error of at most 0.012.
The reference program's roundings to bfloat16 on the way (of `source`, `target` and `weights`) count: a program that leaves them out, or rounds other values in their place, can miss the bound.
Values may be sent and summed in bfloat16 or wider, within the bound.
A program may use at most 128 MiB of HBM per device.

```python
import math
import jax
import jax.numpy as jnp
from jax import lax

D = 1024
H = 4
HS = 256
BS = 128
CELL_CAPACITY = 8
BLK = 1
NB = 32
NODES = 4096
N_ROW = 8
N_COL = 4


def pair_table(key):
    starting_index = jax.random.fold_in(key, 4099)
    selection_seed, tally_seed, clumping_seed = jax.random.split(starting_index, 3)
    span_row = N_COL * BLK
    span_col = N_ROW * BLK
    total = span_row * span_col
    grid_rows = jnp.arange(N_ROW, dtype=jnp.int32).reshape(N_ROW, 1, 1, 1)
    grid_cols = jnp.arange(N_COL, dtype=jnp.int32).reshape(1, N_COL, 1, 1)
    row_slot = jnp.arange(span_row, dtype=jnp.int32).reshape(1, 1, span_row, 1)
    col_slot = jnp.arange(span_col, dtype=jnp.int32).reshape(1, 1, 1, span_col)
    shape = (N_ROW, N_COL, span_row, span_col)
    first = jnp.broadcast_to(grid_rows * span_row + row_slot, shape).reshape(N_ROW, N_COL, total)
    second = jnp.broadcast_to((col_slot // BLK * N_COL + grid_cols) * BLK + col_slot % BLK, shape).reshape(N_ROW, N_COL, total)
    allowed = (first != second) & ((first < second) != ((first + second) % 2 == 1))
    noise = jax.random.randint(selection_seed, (N_ROW, N_COL, total), 0, 16384, dtype=jnp.int32)
    ranking = noise * total + jnp.arange(total, dtype=jnp.int32) + allowed.astype(jnp.int32) * (1 << 30)
    ranked, picked = lax.top_k(ranking, CELL_CAPACITY)
    first_pick = jnp.take_along_axis(first, picked, axis=2)
    second_pick = jnp.take_along_axis(second, picked, axis=2)
    listed = jnp.stack([first_pick, second_pick], axis=-1).astype(jnp.int32)
    room = jnp.sum(allowed.astype(jnp.int32), axis=2)
    couple_tallies = jax.random.randint(tally_seed, (N_ROW, N_COL), 0, 5, dtype=jnp.int32)
    clustered_couples = jax.random.randint(clumping_seed, (N_ROW, N_COL), 0, 8, dtype=jnp.int32) == 0
    couple_tallies = jnp.where(clustered_couples, CELL_CAPACITY, couple_tallies)
    couple_tallies = couple_tallies.at[0, 0].set(CELL_CAPACITY)
    couple_tallies = jnp.minimum(couple_tallies, room).astype(jnp.int32)
    return (listed, couple_tallies)


def draw_pair_blocks(key, part):
    listed, couple_tallies = pair_table(key)
    return listed


def draw_pair_count(key, part):
    listed, couple_tallies = pair_table(key)
    return couple_tallies


def draw_attn(key, part):
    values = jax.random.normal(jax.random.fold_in(key, 11), (H, HS), jnp.float32) * (2.0 / math.sqrt(HS))
    return values


def place_ends(values, key, smallest, high):
    index_at = [jax.random.randint(jax.random.fold_in(key, axis), (), 0, length) for axis, length in enumerate(values.shape)]
    longest = values.shape.index(max(values.shape))
    beside = index_at[:longest] + [(index_at[longest] + 1) % values.shape[longest]] + index_at[longest + 1:]
    return values.at[tuple(index_at)].set(smallest).at[tuple(beside)].set(high)


def level_of(stream_key, extent, cuts, low, largest):
    def one(axis_at, blocks):
        heights = jax.random.uniform(jax.random.fold_in(jax.random.fold_in(stream_key, 6), axis_at), (blocks,), jnp.float32, low / len(cuts), largest / len(cuts))
        return jnp.repeat(jnp.exp(heights), extent[axis_at] // blocks).reshape((-1,) + (1,) * (len(extent) - axis_at - 1))

    factor_of = one(*cuts[0])
    for cut in cuts[1:]:
        factor_of = factor_of * one(*cut)
    return factor_of


def centred(own_key, shape, scale, most, cuts=(), kind=jnp.bfloat16):
    values = jax.random.normal(own_key, shape, jnp.float32) * scale
    if len(cuts) > 0:
        values = level_of(own_key, shape, cuts, -0.22, 0.18) * values
    return jnp.clip(values, min=-most, max=most).astype(kind)


def setup_inputs(seed: int = 0) -> dict:
    key_of = jax.random.split(jax.random.key(seed), 11)
    return {
        "features": centred(key_of[0], (NODES, D), 1.0, 6.0, ((0, 32),)),
        "node_valid": place_ends((jax.random.randint(key_of[1], (NB, BS), 0, 8) < 7).astype(jnp.int32), jax.random.fold_in(key_of[1], 1), 0, 1),
        "self_mask": place_ends((jax.random.randint(key_of[2], (NB, BS, BS), 0, 8) < 1).astype(jnp.int32), jax.random.fold_in(key_of[2], 1), 0, 1),
        "pair_blocks": draw_pair_blocks(jax.random.fold_in(key_of[10], 71), 0),
        "pair_count": draw_pair_count(jax.random.fold_in(key_of[10], 71), 0),
        "pair_masks": place_ends((jax.random.randint(key_of[5], (N_ROW, N_COL, CELL_CAPACITY, BS, BS), 0, 8) < 1).astype(jnp.int32), jax.random.fold_in(key_of[5], 1), 0, 1),
        "weight_src": centred(key_of[6], (D, D), D ** -0.5, 0.1875),
        "weight_tgt": centred(key_of[7], (D, D), D ** -0.5, 0.1875),
        "attn": draw_attn(jax.random.fold_in(key_of[10], 71), 0),
        "bias": centred(key_of[9], (D,), 1.0, 6.0, (), jnp.float32),
    }


FLOOR = -1.0e30


def score_block(target, source, attn):
    heads = attn.shape[0]
    head_width = attn.shape[1]
    target_heads = target.reshape(target.shape[0], heads, head_width)
    source_heads = source.reshape(source.shape[0], heads, head_width)
    planes = []
    for head in range(heads):
        mixed = target_heads[:, head, :].astype(jnp.float32)[:, None, :] + source_heads[:, head, :].astype(jnp.float32)[None, :, :]
        planes.append(jnp.sum(jax.nn.leaky_relu(mixed, 0.2) * attn[head], axis=-1))
    return jnp.stack(planes)


def weigh(weights, source, heads):
    nodes = source.shape[0]
    source_heads = source.reshape(nodes, heads, source.shape[1] // heads).astype(jnp.float32)
    rounded = weights.astype(jnp.bfloat16).astype(jnp.float32)
    mixed = jnp.einsum("hts,shd->thd", rounded, source_heads, precision=lax.Precision.HIGHEST)
    return mixed.reshape(weights.shape[1], source.shape[1])


def to_wire(value):
    return lax.optimization_barrier(value.astype(jnp.bfloat16)).astype(jnp.float32)


def reference(features, node_valid, self_mask, pair_blocks, pair_count, pair_masks, weight_src, weight_tgt, attn, bias):
    blocks = node_valid.shape[0]
    block_size = node_valid.shape[1]
    width = features.shape[1]
    heads = attn.shape[0]
    head_width = attn.shape[1]
    source_all = jnp.dot(features, weight_src, preferred_element_type=jnp.float32).astype(jnp.bfloat16).reshape(blocks, block_size, width)
    target_all = jnp.dot(features, weight_tgt, preferred_element_type=jnp.float32).astype(jnp.bfloat16).reshape(blocks, block_size, width)
    valid = node_valid > 0
    span_row = N_COL * BLK
    span_col = N_ROW * BLK
    flat_blocks = pair_blocks.reshape(-1, 2)
    flat_masks = pair_masks.reshape(-1, block_size, block_size)
    slot_ids = jnp.arange(CELL_CAPACITY, dtype=jnp.int32)
    live = (slot_ids[None, None, :] < pair_count[:, :, None]).reshape(-1)

    def both(item):
        first = flat_blocks[item, 0]
        second = flat_blocks[item, 1]
        adjacency = (flat_masks[item] > 0) & valid[first][:, None] & valid[second][None, :]
        forward = jnp.where(adjacency[None], score_block(target_all[first], source_all[second], attn), FLOOR)
        backward = jnp.where(adjacency.T[None], score_block(target_all[second], source_all[first], attn), FLOOR)
        return first, second, adjacency, forward, backward

    def max_pass(item, carry):
        def live_step(state):
            first, second, adjacency, forward, backward = both(item)
            return (state[0].at[first].max(jnp.max(forward, axis=-1)), state[1].at[second].max(jnp.max(backward, axis=-1)))
        return lax.cond(live[item], live_step, lambda state: state, carry)

    start_peak = jnp.full((blocks, heads, block_size), FLOOR, jnp.float32)
    row_peak, col_peak = lax.fori_loop(0, flat_blocks.shape[0], max_pass, (start_peak, start_peak))

    def cell_pass(cell, totals):
        grid_row = cell // N_COL
        grid_col = cell % N_COL

        def slot_pass(slot, parts):
            item = cell * CELL_CAPACITY + slot

            def live_step(state):
                first, second, adjacency, forward, backward = both(item)
                row_slot = first - grid_row * span_row
                col_slot = (second // BLK) // N_COL * BLK + second % BLK
                weights_fwd = jnp.where(adjacency[None], jnp.exp(forward - row_peak[first][:, :, None]), 0.0)
                weights_bwd = jnp.where(adjacency.T[None], jnp.exp(backward - col_peak[second][:, :, None]), 0.0)
                numer_fwd = weigh(weights_fwd, source_all[second], heads)
                numer_bwd = weigh(weights_bwd, source_all[first], heads)
                return (state[0].at[row_slot].add(numer_fwd), state[1].at[row_slot].add(jnp.sum(weights_fwd, axis=-1)),
                        state[2].at[col_slot].add(numer_bwd), state[3].at[col_slot].add(jnp.sum(weights_bwd, axis=-1)))
            return lax.cond(live[item], live_step, lambda state: state, parts)

        parts = (jnp.zeros((span_row, block_size, width), jnp.float32), jnp.zeros((span_row, heads, block_size), jnp.float32),
                 jnp.zeros((span_col, block_size, width), jnp.float32), jnp.zeros((span_col, heads, block_size), jnp.float32))
        parts = lax.fori_loop(0, CELL_CAPACITY, slot_pass, parts)
        row_numer = totals[0].at[grid_row].add(to_wire(parts[0]).reshape(N_COL, BLK, block_size, width))
        row_denom = totals[1].at[grid_row].add(to_wire(parts[1]).reshape(N_COL, BLK, heads, block_size))
        col_numer = totals[2].at[:, grid_col].add(to_wire(parts[2]).reshape(N_ROW, BLK, block_size, width))
        col_denom = totals[3].at[:, grid_col].add(to_wire(parts[3]).reshape(N_ROW, BLK, heads, block_size))
        return (row_numer, row_denom, col_numer, col_denom)

    totals = (jnp.zeros((N_ROW, N_COL, BLK, block_size, width), jnp.float32), jnp.zeros((N_ROW, N_COL, BLK, heads, block_size), jnp.float32),
              jnp.zeros((N_ROW, N_COL, BLK, block_size, width), jnp.float32), jnp.zeros((N_ROW, N_COL, BLK, heads, block_size), jnp.float32))
    totals = lax.fori_loop(0, N_ROW * N_COL, cell_pass, totals)
    row_numer = totals[0].reshape(blocks, block_size, width)
    row_denom = totals[1].reshape(blocks, heads, block_size)
    col_numer = totals[2].reshape(blocks, block_size, width)
    col_denom = totals[3].reshape(blocks, heads, block_size)
    identity = jnp.eye(block_size, dtype=bool)

    def finish(block):
        flags = valid[block]
        adjacency = ((self_mask[block] > 0) | identity) & flags[:, None] & flags[None, :]
        scores = jnp.where(adjacency[None], score_block(target_all[block], source_all[block], attn), FLOOR)
        top = jnp.maximum(jnp.maximum(row_peak[block], col_peak[block]), jnp.max(scores, axis=-1))
        weights = jnp.where(adjacency[None], jnp.exp(scores - top[:, :, None]), 0.0)
        own = weigh(weights, source_all[block], heads).reshape(block_size, heads, head_width)
        row_scale = jnp.exp(row_peak[block] - top)
        col_scale = jnp.exp(col_peak[block] - top)
        numer = own + row_numer[block].reshape(block_size, heads, head_width) * row_scale.T[:, :, None]
        numer = numer + col_numer[block].reshape(block_size, heads, head_width) * col_scale.T[:, :, None]
        denom = jnp.sum(weights, axis=-1) + row_denom[block] * row_scale + col_denom[block] * col_scale
        denom = denom + (1.0 - flags.astype(jnp.float32))[None, :]
        result = (numer / denom.T[:, :, None]).reshape(block_size, width) + bias[None, :]
        return result.astype(jnp.bfloat16)

    return lax.map(finish, jnp.arange(blocks, dtype=jnp.int32)).reshape(blocks * block_size, width)
```

```python
import functools

import jax
import jax.numpy as jnp
from jax import lax
from jax.experimental import pallas as pl
from jax.experimental.pallas import tpu as pltpu
from jax.sharding import PartitionSpec as P

FLOOR = -1e30
VECTOR_ROWS = 8


def score_block(target, source, attn):
    heads = attn.shape[0]
    head_width = attn.shape[1]
    target_heads = target.reshape(target.shape[0], heads, head_width)
    source_heads = source.reshape(source.shape[0], heads, head_width)
    planes = []
    for head in range(heads):
        mixed = (
            target_heads[:, head, :].astype(jnp.float32)[:, None, :]
            + source_heads[:, head, :].astype(jnp.float32)[None, :, :]
        )
        planes.append(jnp.sum(jax.nn.leaky_relu(mixed, 0.2) * attn[head], axis=-1))
    return jnp.stack(planes)


def weigh(weights, source, heads):
    nodes = source.shape[0]
    source_heads = source.reshape(nodes, heads, source.shape[1] // heads)
    mixed = jnp.einsum(
        "hts,shd->thd",
        weights.astype(jnp.bfloat16),
        source_heads,
        preferred_element_type=jnp.float32,
    )
    return mixed.reshape(weights.shape[1], source.shape[1])


def raise_at(table, position, values):
    current = lax.dynamic_index_in_dim(table, position, 0, keepdims=False)
    return lax.dynamic_update_index_in_dim(table, jnp.maximum(current, values), position, 0)


def add_index(table, position, values):
    current = lax.dynamic_index_in_dim(table, position, 0, keepdims=False)
    return lax.dynamic_update_index_in_dim(table, current + values, position, 0)


def add_rows(table, start, values):
    current = lax.dynamic_slice_in_dim(table, start, values.shape[0], 0)
    return lax.dynamic_update_slice_in_dim(table, current + values, start, 0)


def general_body(
    features,
    node_valid,
    self_mask,
    pair_blocks,
    pair_count,
    pair_masks,
    weight_src,
    weight_tgt,
    attn,
    bias,
):
    owned = node_valid.shape[0]
    block_size = node_valid.shape[1]
    width = features.shape[1]
    heads = attn.shape[0]
    head_width = attn.shape[1]
    row_devices = lax.axis_size("row")
    col_devices = lax.axis_size("col")
    my_row = lax.axis_index("row")
    my_col = lax.axis_index("col")
    valid_flags = node_valid.astype(jnp.bfloat16)
    source_own = jnp.dot(features, weight_src, preferred_element_type=jnp.float32).astype(
        jnp.bfloat16
    )
    target_own = jnp.dot(features, weight_tgt, preferred_element_type=jnp.float32).astype(
        jnp.bfloat16
    )
    packed = jnp.concatenate([source_own, target_own], axis=1)
    row_store, row_valid = (
        lax.all_gather(packed, "col", axis=0, tiled=True),
        lax.all_gather(valid_flags, "col", axis=0, tiled=True),
    )
    col_store, col_valid = (
        lax.all_gather(packed, "row", axis=0, tiled=True),
        lax.all_gather(valid_flags, "row", axis=0, tiled=True),
    )

    def fetch(store, flags, position):
        rows = lax.dynamic_slice_in_dim(store, position * block_size, block_size, 0)
        return (
            rows[:, :width],
            rows[:, width:],
            lax.dynamic_index_in_dim(flags, position, 0, keepdims=False),
        )

    span_row = col_devices * owned
    span_col = row_devices * owned
    live_count = pair_count[0, 0]
    row_peak = jnp.full((span_row, heads, block_size), FLOOR, jnp.float32)
    col_peak = jnp.full((span_col, heads, block_size), FLOOR, jnp.float32)
    kept = []
    for slot in range(pair_blocks.shape[2]):
        first = pair_blocks[0, 0, slot, 0]
        second = pair_blocks[0, 0, slot, 1]
        row_slot = first - my_row * span_row
        col_slot = second // owned // col_devices * owned + second % owned
        is_live = slot < live_count

        def live_scores(operand):
            row_at, col_at, pair_mask = operand
            source_first, target_first, flags_first = fetch(row_store, row_valid, row_at)
            source_second, target_second, flags_second = fetch(col_store, col_valid, col_at)
            adjacency = (pair_mask > 0) & (flags_first[:, None] > 0) & (flags_second[None, :] > 0)
            forward = jnp.where(
                adjacency[None], score_block(target_first, source_second, attn), FLOOR
            )
            backward = jnp.where(
                adjacency.T[None], score_block(target_second, source_first, attn), FLOOR
            )
            return (adjacency, forward, backward, source_first, source_second)

        def dead_scores(operand):
            adjacency = jnp.zeros((block_size, block_size), bool)
            blank = jnp.full((heads, block_size, block_size), FLOOR, jnp.float32)
            empty = jnp.zeros((block_size, width), jnp.bfloat16)
            return (adjacency, blank, blank, empty, empty)

        adjacency, forward, backward, source_first, source_second = lax.cond(
            is_live, live_scores, dead_scores, (row_slot, col_slot, pair_masks[0, 0, slot])
        )
        row_peak = raise_at(row_peak, row_slot, jnp.max(forward, axis=-1))
        col_peak = raise_at(col_peak, col_slot, jnp.max(backward, axis=-1))
        kept.append(
            (is_live, row_slot, col_slot, adjacency, forward, backward, source_first, source_second)
        )
    row_peak = lax.pmax(row_peak.astype(jnp.bfloat16), "col").astype(row_peak.dtype)
    col_peak = lax.pmax(col_peak.astype(jnp.bfloat16), "row").astype(col_peak.dtype)
    row_numer = jnp.zeros((span_row * block_size, width), jnp.float32)
    row_denom = jnp.zeros((span_row, heads, block_size), jnp.float32)
    col_numer = jnp.zeros((span_col * block_size, width), jnp.float32)
    col_denom = jnp.zeros((span_col, heads, block_size), jnp.float32)
    for (
        is_live,
        row_slot,
        col_slot,
        adjacency,
        forward,
        backward,
        source_first,
        source_second,
    ) in kept:
        peak_first = lax.dynamic_index_in_dim(row_peak, row_slot, 0, keepdims=False)
        peak_second = lax.dynamic_index_in_dim(col_peak, col_slot, 0, keepdims=False)

        def live_terms(operand):
            mask_now, fwd, bwd, src_first, src_second, top_first, top_second = operand
            weights_fwd = jnp.where(mask_now[None], jnp.exp(fwd - top_first[:, :, None]), 0.0)
            weights_bwd = jnp.where(mask_now.T[None], jnp.exp(bwd - top_second[:, :, None]), 0.0)
            return (
                weigh(weights_fwd, src_second, heads),
                weigh(weights_bwd, src_first, heads),
                jnp.sum(weights_fwd, axis=-1),
                jnp.sum(weights_bwd, axis=-1),
            )

        def dead_terms(operand):
            rows_zero = jnp.zeros((block_size, width), jnp.float32)
            sums_zero = jnp.zeros((heads, block_size), jnp.float32)
            return (rows_zero, rows_zero, sums_zero, sums_zero)

        numer_fwd, numer_bwd, denom_fwd, denom_bwd = lax.cond(
            is_live,
            live_terms,
            dead_terms,
            (adjacency, forward, backward, source_first, source_second, peak_first, peak_second),
        )
        row_numer = add_rows(row_numer, row_slot * block_size, numer_fwd)
        col_numer = add_rows(col_numer, col_slot * block_size, numer_bwd)
        row_denom = add_index(row_denom, row_slot, denom_fwd)
        col_denom = add_index(col_denom, col_slot, denom_bwd)
    row_numer, row_denom = (
        lax.psum_scatter(
            row_numer.astype(jnp.bfloat16), "col", scatter_dimension=0, tiled=True
        ).astype(jnp.float32),
        lax.psum_scatter(
            row_denom.astype(jnp.bfloat16), "col", scatter_dimension=0, tiled=True
        ).astype(jnp.float32),
    )
    col_numer, col_denom = (
        lax.psum_scatter(
            col_numer.astype(jnp.bfloat16), "row", scatter_dimension=0, tiled=True
        ).astype(jnp.float32),
        lax.psum_scatter(
            col_denom.astype(jnp.bfloat16), "row", scatter_dimension=0, tiled=True
        ).astype(jnp.float32),
    )
    own_row_peak = lax.dynamic_slice_in_dim(row_peak, my_col * owned, owned, 0)
    own_col_peak = lax.dynamic_slice_in_dim(col_peak, my_row * owned, owned, 0)
    identity = jnp.eye(block_size, dtype=bool)
    flags = node_valid[0] > 0
    adjacency = ((self_mask[0] > 0) | identity) & flags[:, None] & flags[None, :]
    scores = jnp.where(adjacency[None], score_block(target_own, source_own, attn), FLOOR)
    top = jnp.maximum(jnp.maximum(own_row_peak[0], own_col_peak[0]), jnp.max(scores, axis=-1))
    weights = jnp.where(adjacency[None], jnp.exp(scores - top[:, :, None]), 0.0)
    own = weigh(weights, source_own, heads).reshape(block_size, heads, head_width)
    row_scale = jnp.exp(own_row_peak[0] - top)
    col_scale = jnp.exp(own_col_peak[0] - top)
    numer = own + row_numer.reshape(block_size, heads, head_width) * row_scale.T[:, :, None]
    numer = numer + col_numer.reshape(block_size, heads, head_width) * col_scale.T[:, :, None]
    denom = jnp.sum(weights, axis=-1) + row_denom[0] * row_scale + col_denom[0] * col_scale
    denom = denom + (1.0 - flags.astype(jnp.float32))[None, :]
    result = (numer / denom.T[:, :, None]).reshape(block_size, width) + bias[None, :]
    results = result.astype(jnp.bfloat16)
    return results


NT = (((1,), (1,)), ((), ()))


def attend_kernel(heads, vector_rows, table, source_in, target_in, masks_in, flags, attn_main, attn_scaled,
                  attn_cols, attn_rows, bias, out, source, target, masks, others, planes, counts,
                  spread_wide, spread_thin, scores, source_term, sems):
    blocks, width, nodes = source.shape
    part = target.shape[1]
    layers = masks.shape[0] // blocks
    slots = (layers - 2) // 2
    half = attn_main.shape[0] // 2
    f32 = jnp.float32
    copies = [
        pltpu.make_async_copy(src, dst, sems.at[at])
        for at, (src, dst) in enumerate([(source_in, source), (target_in, target), (masks_in, masks)])
    ]
    for copy in copies:
        copy.start()

    def own_plane(block):
        return (block % heads * (blocks // heads) + block // heads) * layers + 2 * slots

    def append(block, other, plane):
        at = counts[block]
        others[block, at] = other
        planes[block, at] = plane
        counts[block] = at + 1

    def begin(block, carry):
        counts[block] = 0
        append(block, block, own_plane(block))
        return carry

    lax.fori_loop(0, blocks, begin, 0)

    def cell(index, carry):
        def pair(slot, inner):
            first = table[index, 2 * slot]
            second = table[index, 2 * slot + 1]
            append(first, second, index * layers + slot)
            append(second, first, index * layers + slots + slot)
            return inner

        return lax.fori_loop(0, table[index, 2 * slots], pair, carry)

    lax.fori_loop(0, blocks, cell, 0)

    def pad(block, carry):
        for step in range(3):
            others[block, counts[block] + step] = block
            planes[block, counts[block] + step] = own_plane(block)
        return carry

    lax.fori_loop(0, blocks, pad, 0)
    for copy in copies:
        copy.wait()

    def project(lhs, values):
        both = jnp.dot(lhs, values, preferred_element_type=f32)
        return both[:half] + both[half:]

    def prepare(step, carry):
        for more in range(4):
            source_term[step * 4 + more] = project(attn_main[...], source[step * 4 + more])
        return carry

    lax.fori_loop(0, blocks // 4, prepare, 0)
    index = lax.broadcasted_iota(jnp.int32, (half, nodes), 0)

    def mixed_scores(other):
        sums = [jnp.zeros((half, nodes), f32) for _ in range(vector_rows)]
        tiles = [jnp.zeros((half, nodes), f32) for _ in range(part // half)]
        for at in range(vector_rows, part, 2):
            values = source[other]
            mixed = jnp.concatenate(
                [
                    jnp.minimum(spread_thin[at - vector_rows], values),
                    jnp.minimum(spread_thin[at + 1 - vector_rows], values),
                ],
                axis=1,
            )
            both = project(attn_scaled[...], mixed)
            for more in range(2):
                tile = (at + more) // half
                tiles[tile] = jnp.where(
                    index == (at + more) % half, both[:, more * nodes : (more + 1) * nodes], tiles[tile])
        for base in range(0, width, 2 * half):
            values = source[other, base : base + 2 * half, :].astype(f32)
            for low in range(0, 2 * half, half):
                scale = attn_cols[base + low : base + low + half, :]
                value = values[low : low + half]
                for at in range(vector_rows):
                    spread = spread_wide[at, base + low : base + low + half, :]
                    sums[at] = sums[at] + scale * jnp.minimum(spread, value)
        for at in range(vector_rows):
            total = jnp.broadcast_to(jnp.sum(sums[at], axis=0, keepdims=True), (half, nodes))
            tiles[at // half] = jnp.where(index == at % half, total, tiles[at // half])
        return jnp.concatenate(tiles, axis=0)

    def one_block(block, carry):
        rows = target[block].astype(f32)
        term = jnp.sum(rows * attn_rows[...], axis=1, keepdims=True)
        turned = jnp.concatenate([rows, jnp.zeros((nodes - part, width), f32)], axis=0).T
        for at in range(part):
            plane = jnp.broadcast_to(turned[:, at : at + 1], (width, nodes))
            if at < vector_rows:
                spread_wide[at] = plane
            else:
                spread_thin[at - vector_rows] = plane.astype(spread_thin.dtype)
        count = counts[block]
        turns = (count + 1) // 2

        def score(step, best):
            for more in range(2):
                at = 2 * step + more
                other = others[block, at]
                values = mixed_scores(other) + term + source_term[other][:1, :]
                limit = jnp.where(at < count, 0.0, 2.0)
                keep = masks[planes[block, at]].astype(f32) * flags[other] > limit
                values = jnp.where(keep, values, FLOOR)
                scores[at] = values
                best = jnp.maximum(best, values)
            return best

        best = lax.fori_loop(0, turns, score, jnp.full((part, nodes), FLOOR, f32))
        for more in range(2):
            scores[2 * turns + more] = jnp.full((part, nodes), FLOOR, f32)
        peak = jnp.max(best, axis=1, keepdims=True)

        def weigh(step, state):
            total, numer = state
            for more in range(0, 4, 2):
                at = 4 * step + more
                weights = [jnp.exp(scores[at + extra] - peak) for extra in range(2)]
                total = total + weights[0] + weights[1]
                values = [source[others[block, at + extra]] for extra in range(2)]
                numer = numer + lax.dot_general(
                    jnp.concatenate(weights, axis=1).astype(jnp.bfloat16),
                    jnp.concatenate(values, axis=1), NT, preferred_element_type=f32)
            return total, numer

        total, numer = lax.fori_loop(
            0, (count + 3) // 4, weigh, (jnp.zeros((part, nodes), f32), jnp.zeros((part, width), f32)))
        sums = jnp.sum(total, axis=1, keepdims=True)
        out[block] = (numer / sums + bias[...]).astype(out.dtype)
        return carry

    lax.fori_loop(0, blocks, one_block, 0)


def attend(heads, vector_rows, table, source, target, masks, flags, attn_head, bias_head):
    blocks, width, nodes = source.shape
    part = target.shape[1]
    half = 8
    bf16, f32 = jnp.bfloat16, jnp.float32
    vmem = pl.BlockSpec(memory_space=pltpu.VMEM)
    anywhere = pl.BlockSpec(memory_space=pl.ANY)
    smem = pltpu.SMEM
    return pl.pallas_call(
        functools.partial(attend_kernel, heads, vector_rows),
        out_shape=jax.ShapeDtypeStruct((blocks, part, width), bf16),
        in_specs=[pl.BlockSpec(memory_space=pltpu.SMEM)] + [anywhere] * 3 + [vmem] * 6,
        out_specs=vmem,
        scratch_shapes=[
            pltpu.VMEM(source.shape, bf16),
            pltpu.VMEM(target.shape, bf16),
            pltpu.VMEM(masks.shape, bf16),
            smem((blocks, blocks + 4), jnp.int32),
            smem((blocks, blocks + 4), jnp.int32),
            smem((blocks,), jnp.int32),
            pltpu.VMEM((vector_rows, width, nodes), f32),
            pltpu.VMEM((part - vector_rows, width, nodes), bf16),
            pltpu.VMEM((blocks + 4, part, nodes), f32),
            pltpu.VMEM((blocks, half, nodes), f32),
            pltpu.SemaphoreType.DMA((3,)),
        ],
        compiler_params=pltpu.CompilerParams(vmem_limit_bytes=40 * 2**20),
    )(
        table,
        source,
        target,
        masks,
        flags,
        split_pair(attn_head, half),
        split_pair(-0.8 * attn_head, half),
        jnp.broadcast_to((-0.8 * attn_head).reshape(width, 1), (width, nodes)),
        -0.2 * attn_head,
        bias_head,
    )


def split_pair(values, half):
    main = values.astype(jnp.bfloat16)
    rest = (values - main.astype(jnp.float32)).astype(jnp.bfloat16)
    shape = (half, values.shape[-1])
    return jnp.concatenate([jnp.broadcast_to(main, shape), jnp.broadcast_to(rest, shape)], axis=0)


MESH = pl.DeviceIdType.MESH


def exchange_kernel(heads, depth, masks_in, source_in, target_in, masks, source, target,
                    sems_m1, sems_m2, sems_src, sems_z, sems_sib, sems_tgt, local):
    row, z = lax.axis_index("row"), lax.axis_index("col")
    p, k = row // 2, row % 2
    barrier = pltpu.get_barrier_semaphore()
    others = [(dp, dk, dz) for dz in range(depth) for dp in range(heads) for dk in range(2)][1:]

    def place(dp, dk, dz):
        return lax.rem(p + dp, heads), lax.rem(k + dk, 2), lax.rem(z + dz, depth)

    def device(there):
        return (there[0] * 2 + there[1], there[2])

    for step in others:
        pl.semaphore_signal(barrier, inc=1, device_id=device(place(*step)), device_id_type=MESH)
    pl.semaphore_wait(barrier, len(others))

    sent = []

    def send(src, dst, sems, out_at, in_at, there):
        copy = pltpu.make_async_remote_copy(
            src_ref=src, dst_ref=dst, send_sem=sems.at[(0,) + out_at], recv_sem=sems.at[(1,) + in_at],
            device_id=device(there), device_id_type=MESH)
        copy.start()
        return copy

    def arrive(dst, sems, in_at):
        pltpu.make_async_remote_copy(
            src_ref=dst, dst_ref=dst, send_sem=sems.at[(1,) + in_at], recv_sem=sems.at[(1,) + in_at],
            device_id=device(place(1, 0, 0)), device_id_type=MESH).wait_recv()

    for dz in (1, depth - 1) + tuple(range(2, depth - 1)) + (0,):
        for dk in range(2):
            if (dz, dk) == (0, 0):
                continue
            there = place(0, dk, dz)
            sent.append(send(masks_in.at[there[2], there[1]], masks.at[p, z, k], sems_m1,
                             (dz, dk), (z, k), there))
    own_m = pltpu.make_async_copy(masks_in.at[z, k], masks.at[p, z, k], local.at[0])
    own_s = pltpu.make_async_copy(source_in.at[p], source.at[z, k, p], local.at[1])
    own_t = pltpu.make_async_copy(target_in.at[p, z, k], target.at[z, k, p], local.at[2])
    own_m.start()
    own_s.start()
    own_t.start()
    for dp in range(1, heads):
        there = place(dp, 0, 0)
        sent.append(send(source_in.at[there[0]], source.at[z, k, p], sems_src, (dp,), (p,), there))
    for dp, dk, dz in others:
        there = place(dp, dk, dz)
        sent.append(send(target_in.at[there[0], there[2], there[1]], target.at[z, k, p], sems_tgt,
                         (dz, dk, dp), (z, k, p), there))

    def spread(dz):
        at = lax.rem(z + dz, depth)
        for dp in range(1, heads):
            there = place(dp, 0, 0)
            sent.append(send(masks.at[p, at], masks.at[p, at], sems_m2, (dp, dz), (p, at), there))

    sibling = place(0, 1, 0)

    def beside(at):
        return send(source.at[at, k], source.at[at, k], sems_sib, (at,), (at,), sibling)

    own_m.wait()
    arrive(masks.at[p, z, 1 - k], sems_m1, (z, 1 - k))
    spread(0)

    own_s.wait()
    for dp in range(1, heads):
        there = place(dp, 0, 0)
        arrive(source.at[z, k, there[0]], sems_src, (there[0],))

    def pass_on(at, up):
        there = (p, k, z + 1) if up else (p, k, z - 1)
        return pltpu.make_async_remote_copy(
            src_ref=source.at[at, k], dst_ref=source.at[at, k],
            send_sem=sems_z.at[0, 1 if up else 0, at], recv_sem=sems_z.at[1, 0, at],
            device_id=device(there), device_id_type=MESH)

    @pl.when(z < depth - 1)
    def _():
        pass_on(z, True).start()

    @pl.when(z > 0)
    def _():
        pass_on(z, False).start()

    sent.append(beside(z))

    for d in range(1, depth):
        for dz in (d, depth - d):
            if d <= depth - d and not (d == depth - d and dz != d):
                at = lax.rem(z + dz, depth)
                for kk in range(2):
                    arrive(masks.at[p, at, kk], sems_m1, (at, kk))
                spread(dz)
                if d == depth - d:
                    break

        @pl.when(z >= d)
        def _():
            arrive(source.at[z - d, k], sems_z, (0, z - d))

            @pl.when(z < depth - 1)
            def _():
                pass_on(z - d, True).start()

            beside(z - d)

        @pl.when(z + d < depth)
        def _():
            arrive(source.at[z + d, k], sems_z, (0, z + d))

            @pl.when(z > 0)
            def _():
                pass_on(z + d, False).start()

            beside(z + d)

    for dz in range(depth):
        at = lax.rem(z + dz, depth)
        for dp in range(1, heads):
            there = place(dp, 0, 0)
            arrive(masks.at[there[0], at], sems_m2, (there[0], at))
        arrive(source.at[at, 1 - k], sems_sib, (at,))
    own_t.wait()
    for dp, dk, dz in others:
        there = place(dp, dk, dz)
        arrive(target.at[there[2], there[1], there[0]], sems_tgt, (there[2], there[1], there[0]))
    for copy in sent:
        copy.wait_send()
    for d in range(0, depth):
        @pl.when((z >= d) & (z < depth - 1))
        def _():
            pass_on(z - d, True).wait_send()

        @pl.when((z + d < depth) & (z > 0))
        def _():
            pass_on(z + d, False).wait_send()

        if d > 0:
            at = lax.rem(z + d, depth)
            pltpu.make_async_remote_copy(
                src_ref=source.at[at, k], dst_ref=source.at[at, k], send_sem=sems_sib.at[0, at],
                recv_sem=sems_sib.at[1, at], device_id=device(sibling), device_id_type=MESH).wait_send()


def collect_kernel(heads, depth, parts, out, sems, local):
    row, z = lax.axis_index("row"), lax.axis_index("col")
    p, k = row // 2, row % 2
    barrier = pltpu.get_barrier_semaphore()
    others = [(dp, dk, dz) for dz in range(depth) for dp in range(heads) for dk in range(2)][1:]

    def place(dp, dk, dz):
        return lax.rem(p + dp, heads), lax.rem(k + dk, 2), lax.rem(z + dz, depth)

    for step in others:
        there = place(*step)
        pl.semaphore_signal(barrier, inc=1, device_id=(there[0] * 2 + there[1], there[2]), device_id_type=MESH)
    pl.semaphore_wait(barrier, len(others))
    own = pltpu.make_async_copy(parts.at[z, k, p], out.at[p, z, k], local.at[0])
    own.start()
    sent = []
    for dp, dk, dz in others:
        there = place(dp, dk, dz)
        copy = pltpu.make_async_remote_copy(
            src_ref=parts.at[there[2], there[1], there[0]], dst_ref=out.at[p, z, k],
            send_sem=sems.at[0, dp, dz, dk], recv_sem=sems.at[1, p, z, k],
            device_id=(there[0] * 2 + there[1], there[2]), device_id_type=MESH)
        copy.start()
        sent.append(copy)
    own.wait()
    for dp, dk, dz in others:
        there = place(dp, dk, dz)
        dst = out.at[there[0], there[2], there[1]]
        sem = sems.at[1, there[0], there[2], there[1]]
        pltpu.make_async_remote_copy(
            src_ref=dst, dst_ref=dst, send_sem=sem, recv_sem=sem,
            device_id=(there[0] * 2 + there[1], there[2]), device_id_type=MESH).wait_recv()
    for copy in sent:
        copy.wait_send()


def sliced_body(features, node_valid, self_mask, pair_blocks, pair_count, pair_masks,
                weight_src, weight_tgt, attn, bias):
    nodes = node_valid.shape[1]
    width = features.shape[1]
    heads, head_width = attn.shape
    depth = lax.axis_size("col")
    my_head = lax.axis_index("row") // 2
    blocks = lax.axis_size("row") * depth
    slices = 2 * depth
    part = nodes // slices
    slots = pair_blocks.shape[2]
    bf16 = jnp.bfloat16
    dma = pltpu.SemaphoreType.DMA
    vmem = pl.BlockSpec(memory_space=pltpu.VMEM)

    source_own = lax.dot_general(
        weight_src, features, (((0,), (1,)), ((), ())), preferred_element_type=jnp.float32)
    source_own = source_own.astype(bf16).reshape(heads, head_width, nodes)
    target_own = -jnp.dot(features, weight_tgt, preferred_element_type=jnp.float32)
    target_own = target_own.astype(bf16).reshape(depth, 2, part, heads, head_width).transpose(3, 0, 1, 2, 4)

    pair_mask = (pair_masks[0, 0] > 0).astype(bf16)
    own_mask = ((self_mask > 0) | jnp.eye(nodes, dtype=bool)[None]).astype(bf16)
    small = jnp.concatenate(
        [node_valid.reshape(1, -1), pair_blocks.reshape(1, -1), pair_count.reshape(1, 1)], axis=1
    ).astype(bf16)
    rows_small = -(-small.shape[1] // nodes)
    small = jnp.pad(small, ((0, 0), (0, part * nodes - small.shape[1]))).reshape(1, part, nodes)
    stacked = jnp.concatenate([pair_mask, pair_mask.transpose(0, 2, 1), own_mask], axis=0)
    stacked = stacked.reshape(-1, slices, part, nodes).transpose(1, 0, 2, 3)
    stacked = jnp.concatenate([stacked, jnp.broadcast_to(small[None], (slices, 1, part, nodes))], axis=1)
    layers = stacked.shape[1]
    stacked = stacked.reshape(depth, 2, layers, part, nodes)

    masks, source_all, target_all = pl.pallas_call(
        functools.partial(exchange_kernel, heads, depth),
        out_shape=[
            jax.ShapeDtypeStruct((heads, depth, 2, layers, part, nodes), bf16),
            jax.ShapeDtypeStruct((depth, 2, heads, head_width, nodes), bf16),
            jax.ShapeDtypeStruct((depth, 2, heads, part, head_width), bf16),
        ],
        in_specs=[vmem] * 3,
        out_specs=[vmem] * 3,
        scratch_shapes=[
            dma((2, depth, 2)),
            dma((2, heads, depth)),
            dma((2, heads)),
            dma((2, 2, depth)),
            dma((2, depth)),
            dma((2, depth, 2, heads)),
            dma((3,)),
        ],
        compiler_params=pltpu.CompilerParams(
            collective_id=0, has_side_effects=True, vmem_limit_bytes=24 * 2**20),
    )(stacked, source_own, target_own)

    small = masks.reshape(blocks, layers, part, nodes)[:, layers - 1, :rows_small, :]
    small = small.reshape(blocks, rows_small * nodes)
    masks = masks.reshape(blocks * layers, part, nodes)
    source_all = source_all.reshape(blocks, head_width, nodes)
    target_all = target_all.reshape(blocks, part, head_width)
    flags = small[:, :nodes].astype(jnp.float32).reshape(heads, slices, 1, nodes)
    flags = flags.transpose(1, 0, 2, 3).reshape(blocks, 1, nodes)
    table = small[:, nodes : nodes + 2 * slots + 1].astype(jnp.int32)
    at_row, at_col = table // depth, table % depth
    places = (at_col * 2 + at_row % 2) * heads + at_row // 2
    table = jnp.where(jnp.arange(2 * slots + 1) < 2 * slots, places, table)

    attn_head = lax.dynamic_slice_in_dim(attn, my_head, 1, 0)
    bias_head = lax.dynamic_slice_in_dim(bias.reshape(heads, head_width), my_head, 1, 0)
    out = attend(heads, VECTOR_ROWS, table, source_all, target_all, masks, flags, attn_head, bias_head)
    out = pl.pallas_call(
        functools.partial(collect_kernel, heads, depth),
        out_shape=jax.ShapeDtypeStruct((heads, depth, 2, part, head_width), bf16),
        in_specs=[vmem],
        out_specs=vmem,
        scratch_shapes=[dma((2, heads, depth, 2)), dma((1,))],
        compiler_params=pltpu.CompilerParams(collective_id=1, has_side_effects=True),
    )(out.reshape(depth, 2, heads, part, head_width))
    out = out.reshape(heads, nodes, head_width).transpose(1, 0, 2).reshape(nodes, width)
    blank = jnp.broadcast_to(bias[None, :], (nodes, width)).astype(bf16)
    return jnp.where(node_valid.reshape(nodes, 1) > 0, out, blank)


def pick_body(mesh, features, node_valid, *rest):
    heads = rest[-2].shape[0]
    rows, cols = mesh.shape["row"], mesh.shape["col"]
    even = node_valid.shape[0] == 1 and rows == 2 * heads and node_valid.shape[1] % (cols * 32) == 0
    even = even and rows * cols <= 256 and cols > 2
    return (sliced_body if even else general_body)(features, node_valid, *rest)


def solution(mesh):
    return jax.shard_map(
        functools.partial(pick_body, mesh),
        mesh=mesh,
        in_specs=(
            P(("row", "col"), None),
            P(("row", "col"), None),
            P(("row", "col"), None, None),
            P("row", "col", None, None),
            P("row", "col"),
            P("row", "col", None, None, None),
            P(),
            P(),
            P(),
            P(),
        ),
        out_specs=P(("row", "col"), None),
        check_vma=False,
    )
```
